32 devices in a mesh: ta: 8 (over z, y), gx: 4 (over x, core).
Axes of the slice: x: 2, y: 2, z: 4, core: 2. Of those that a mesh axis runs over, the one named last changes fastest.
Arguments:
- right_side: float32 [64, 64, 64, 128], P('ta', 'gx'), may hold values from -6 to 6
- basis_x: float32 [64, 64], replicated, may hold values from -0.75 to 0.75
- basis_y: float32 [64, 64], replicated, may hold values from -0.75 to 0.75
- basis_z: float32 [128, 128], replicated, may hold values from -0.5 to 0.5
- eig_x: float32 [64], replicated, may hold values from 1 to 5.3312
- eig_y: float32 [64], replicated, may hold values from 1 to 5.3312
- eig_z: float32 [128], replicated, may hold values from 1 to 5.3312
- steps: float32 [64], replicated, may hold values from 0.25 to 1
Outputs:
- preconditioned: float32 [64, 64, 64, 128], P('ta', 'gx')
The draws below stay inside these ranges and needn't reach their ends.
All inputs are finite; a program needn't handle non-finite values.
Results may differ from the reference program's by a relative error of at most 0.00012.
Values sent between devices are 32-bit elements; how exact they have to be, the bound alone decides.
A program may use at most 192 MiB of HBM per device.

```python
import math
import jax
import jax.numpy as jnp
from jax import lax

NX = 64
NY = 64
NZ = 128
NT = 64


def steps_of(own_key, extent, split, low, largest):
    gain, own = 1.0, jax.random.fold_in(own_key, 6)
    for axis_at, blocks in split:
        draws = jnp.exp(jax.random.uniform(jax.random.fold_in(own, axis_at), (blocks,), jnp.float32, low / len(split), largest / len(split)))
        gain = gain * jnp.repeat(draws, extent[axis_at] // blocks).reshape([-1 if axis == axis_at else 1 for axis in range(len(extent))])
    return gain


def noise(key, dims, deviation, most, shards=(), held_as=jnp.bfloat16):
    drawn = jax.random.normal(key, dims, jnp.float32) * deviation
    if len(shards) > 0:
        drawn = steps_of(key, dims, shards, -0.22, 0.18) * drawn
    return jnp.clip(drawn, min=-most, max=most).astype(held_as)


def setup_inputs(seed: int = 0) -> dict:
    key_of = jax.random.split(jax.random.key(seed), 9)
    return {
        "right_side": noise(key_of[0], (NT, NX, NY, NZ), 1.0, 6.0, ((0, 8), (1, 4)), jnp.float32),
        "basis_x": noise(key_of[1], (NX, NX), NX ** -0.5, 0.75, (), jnp.float32),
        "basis_y": noise(key_of[2], (NY, NY), NY ** -0.5, 0.75, (), jnp.float32),
        "basis_z": noise(key_of[3], (NZ, NZ), NZ ** -0.5, 0.5, (), jnp.float32),
        "eig_x": jnp.clip(jnp.exp(jax.random.uniform(key_of[4], (NX,), jnp.float32, math.log(1.0), math.log(5.3312))), 1.0, 5.3312),
        "eig_y": jnp.clip(jnp.exp(jax.random.uniform(key_of[5], (NY,), jnp.float32, math.log(1.0), math.log(5.3312))), 1.0, 5.3312),
        "eig_z": jnp.clip(jnp.exp(jax.random.uniform(key_of[6], (NZ,), jnp.float32, math.log(1.0), math.log(5.3312))), 1.0, 5.3312),
        "steps": jnp.clip(jnp.exp(jax.random.uniform(key_of[7], (NT,), jnp.float32, math.log(0.25), math.log(1.0))), 0.25, 1.0),
    }


precise = lax.Precision.HIGHEST

def reference(right_side, basis_x, basis_y, basis_z, eig_x, eig_y, eig_z, steps):

    def forward(time_plane):
        halfway = jnp.einsum('abc,cl->abl', time_plane, basis_z, precision=precise)
        halfway = jnp.einsum('abc,bj->ajc', halfway, basis_y, precision=precise)
        return jnp.einsum('abc,ai->ibc', halfway, basis_x, precision=precise)
    spectral = lax.map(forward, right_side)
    total_rows = steps.shape[0]
    lengths = steps / total_rows
    following = jnp.concatenate([lengths[1:], jnp.zeros((1,), lengths.dtype)])
    position = jnp.arange(total_rows, dtype=jnp.int32)
    closing = jnp.where(position == total_rows - 1, 0.5, 0.0).astype(lengths.dtype)

    def solve_slab(mode_at):
        time_rows = lax.dynamic_index_in_dim(spectral, mode_at, 1, keepdims=False)
        eigen_sum = (eig_x[mode_at] + eig_y[:, None] + eig_z[None, :])[:, :, None]
        sub_diag = jnp.where(position == 0, 0.0, eigen_sum * (lengths / 6.0) - 0.5)
        main_diag = eigen_sum * ((lengths + following) / 3.0) + closing
        super_diag = jnp.where(position == total_rows - 1, 0.0, eigen_sum * (following / 6.0) + 0.5)
        right_rows = jnp.transpose(time_rows, (1, 2, 0))[..., None]
        result = lax.linalg.tridiagonal_solve(sub_diag, main_diag, super_diag, right_rows)[..., 0]
        return jnp.transpose(result, (2, 0, 1))
    solved = lax.map(solve_slab, jnp.arange(NX, dtype=jnp.int32))

    def backward(time_at):
        time_plane = lax.dynamic_index_in_dim(solved, time_at, 1, keepdims=False)
        halfway = jnp.einsum('ibc,ai->abc', time_plane, basis_x, precision=precise)
        halfway = jnp.einsum('ajl,cl->ajc', halfway, basis_z, precision=precise)
        return jnp.einsum('ajc,bj->abc', halfway, basis_y, precision=precise)
    return lax.map(backward, jnp.arange(total_rows, dtype=jnp.int32))
```

```python
from functools import partial

import jax
import jax.numpy as jnp
from jax import lax
from jax.experimental import pallas as pl
from jax.experimental.pallas import tpu as pltpu
from jax.sharding import PartitionSpec as P

MESH = pl.DeviceIdType.MESH
SUB = 8
WAVE = 3
BF = jnp.bfloat16
F32 = jnp.float32


def halves(value):
    high = value.astype(BF)
    low = (value - high.astype(F32)).astype(BF)
    return high, low


def dot(a, b):
    return jnp.dot(a, b, preferred_element_type=F32)


def left(matrix, value):
    high, low = halves(value)
    return dot(matrix, jnp.concatenate([high, low, high], axis=0))


def right(value, twice, rest):
    high, low = halves(value)
    return dot(jnp.concatenate([high, low], axis=1), twice) + dot(high, rest)


def kernel(
    chain, cols, chunks, group,
    x_ref, zf1, zf2, zb1, zb2, yf, yb, xf, xb, exz, eig_y, mains, sixth, square, closing,
    out_ref,
    field, fsend, frecv, modal, rd, w, e, rdb, wb, last, sig, rho, gs, gr, hs, hr, bsend, brecv,
    in_sem, out_sem, fs_sem, fr_sem, fl_sem, bs_sem, br_sem, bl_sem, gs_sem, gr_sem, hs_sem, hr_sem,
):
    pos, me = lax.axis_index("ta"), lax.axis_index("gx")
    rows, block, ny, nz = field.shape
    nx = exz.shape[0]
    span = chunks * SUB
    up, down = lax.rem(pos + 1, chain), lax.rem(pos + chain - 1, chain)

    def load(t):
        return pltpu.make_async_copy(x_ref.at[t], field.at[t], in_sem.at[t])

    for t in range(rows):
        load(t).start()

    barrier = pltpu.get_barrier_semaphore()
    for d in range(1, cols):
        pl.semaphore_signal(barrier, inc=1, device_id={"gx": lax.rem(me + d, cols)}, device_id_type=MESH)
    for other in (up, down):
        pl.semaphore_signal(barrier, inc=1, device_id={"ta": other}, device_id_type=MESH)
    pl.semaphore_wait(barrier, cols + 1)

    def forward_copy(c, g, d, receive):
        times = pl.ds(g * group, group)
        to, here = lax.rem(me + d, cols), me
        if receive:
            to, here = me, lax.rem(me + cols - d, cols)
        return pltpu.make_async_remote_copy(
            src_ref=fsend.at[to, c, times], dst_ref=frecv.at[here, c, times],
            send_sem=fs_sem.at[c, g, d - 1], recv_sem=fr_sem.at[c, g, d - 1],
            device_id={"gx": lax.rem(me + d, cols)}, device_id_type=MESH,
        )

    def forward_own(c, g):
        times = pl.ds(g * group, group)
        return pltpu.make_async_copy(fsend.at[me, c, times], frecv.at[me, c, times], fl_sem.at[c, g])

    def start_forward(c, g):
        for d in range(1, cols):
            forward_copy(c, g, d, False).start()
        forward_own(c, g).start()

    def transform(g, carry):
        for k in range(group):
            t = g * group + k
            load(t).wait()
            for first in range(0, block, 4):
                value = field[t, first : first + 4].reshape(4 * ny, nz)
                value = right(value, zf1[...], zf2[...])
                for a in range(4):
                    y = left(yf[...], value[a * ny : (a + 1) * ny])
                    for q in range(cols):
                        for c in range(chunks):
                            at = (q * chunks + c) * SUB
                            fsend[q, c, t, pl.ds(first + a, SUB, stride=block), :] = y[at : at + SUB]
        start_forward(0, g)
        return carry

    lax.fori_loop(0, rows // group, transform, 0)
    for c in range(1, chunks):
        for g in range(rows // group):
            start_forward(c, g)

    def shift_of(c, j):
        return exz[...] + eig_y[me * span + c * SUB + j]

    def matrices(n, carry):
        c, j = n // SUB, lax.rem(n, SUB)
        s = shift_of(c, j)
        s2 = s * s
        own = pl.ds(pl.multiple_of(j * nx, nx), nx)

        def coupling(k):
            return s2 * square[k] - 0.25

        def before(q, ratio):
            one, two = jnp.ones_like(s), ratio
            for r in range(rows):
                k = q * rows + r
                one, two = (s * mains[k]) * one - coupling(k) * two, one
            return two / one

        def after(n, ratio):
            q = chain - 1 - n
            one, two = jnp.ones_like(s), ratio
            for r in range(rows - 1, -1, -1):
                k = q * rows + r
                one, two = (s * mains[k] + closing[k]) * one - coupling(k + 1) * two, one
            return two / one

        ratio = lax.fori_loop(0, pos, before, jnp.zeros_like(s))
        product = None
        for r in range(rows):
            k = pos * rows + r
            ratio = 1.0 / (s * mains[k] + closing[k] - coupling(k) * ratio)
            rd[c, r, own] = ratio
            weight = (0.5 - s * sixth[k]) * ratio
            w[c, r, own] = weight
            product = weight if product is None else product * weight
            carry_over = (s * sixth[k + 1] + 0.5) * ratio
            e[c, r, own] = carry_over
        sig[c, j] = product
        ratio = lax.fori_loop(0, chain - 1 - pos, after, jnp.zeros_like(s))
        end = pos * rows + rows
        last[c, j] = 1.0 / (1.0 - carry_over * ((s * sixth[end] - 0.5) * ratio))
        product = None
        for r in range(rows - 1, -1, -1):
            k = pos * rows + r
            ratio = 1.0 / (s * mains[k] + closing[k] - coupling(k + 1) * ratio)
            rdb[c, r, own] = ratio
            weight = -(s * sixth[k + 1] + 0.5) * ratio
            wb[c, r, own] = weight
            product = weight if product is None else product * weight
        rho[c, j] = product
        return carry

    lax.fori_loop(0, span, matrices, 0)

    def chain_copy(send, receive, s_sem, r_sem, c, j, other):
        return pltpu.make_async_remote_copy(
            src_ref=send.at[c, j], dst_ref=receive.at[c, j], send_sem=s_sem.at[c, j], recv_sem=r_sem.at[c, j],
            device_id={"ta": other}, device_id_type=MESH,
        )

    def upward(c, j):
        return chain_copy(gs, gr, gs_sem, gr_sem, c, j, up)

    def downward(c, j):
        return chain_copy(hs, hr, hs_sem, hr_sem, c, j, down)

    first, final = pos == 0, pos == chain - 1

    @pl.when(first)
    def _():
        gr[...] = jnp.zeros_like(gr)

    @pl.when(final)
    def _():
        hr[...] = jnp.zeros_like(hr)

    def back_copy(c, j, d, receive):
        to, here = lax.rem(me + d, cols), me
        if receive:
            to, here = me, lax.rem(me + cols - d, cols)
        part = pl.ds(pl.multiple_of(j * rows * block, rows * block), rows * block)
        return pltpu.make_async_remote_copy(
            src_ref=bsend.at[to, c, part], dst_ref=brecv.at[here, c, part],
            send_sem=bs_sem.at[c, j, d - 1], recv_sem=br_sem.at[c, j, d - 1],
            device_id={"gx": lax.rem(me + d, cols)}, device_id_type=MESH,
        )

    def back_own(c, j):
        part = pl.ds(pl.multiple_of(j * rows * block, rows * block), rows * block)
        return pltpu.make_async_copy(bsend.at[me, c, part], brecv.at[me, c, part], bl_sem.at[c, j])

    def chunk(c, carry):
        def arrive(g, carry):
            forward_own(c, g).wait()
            for d in range(1, cols):
                forward_copy(c, g, d, True).wait_recv()
            for k in range(group):
                t = g * group + k
                for j in range(SUB):
                    value = jnp.concatenate(
                        [frecv[q, c, t, j * block : (j + 1) * block, :] for q in range(cols)], axis=0
                    )
                    modal[t, j * nx : (j + 1) * nx] = left(xf[...], value)
            return carry

        lax.fori_loop(0, rows // group, arrive, 0)

        def maps(j, carry):
            own = pl.ds(pl.multiple_of(j * nx, nx), nx)
            g = modal[0, own] * rd[c, 0, own]
            for t in range(1, rows):
                g = modal[t, own] * rd[c, t, own] + w[c, t, own] * g
            gs[c, j] = g
            h = modal[rows - 1, own] * rdb[c, rows - 1, own]
            for t in range(rows - 2, -1, -1):
                h = modal[t, own] * rdb[c, t, own] + wb[c, t, own] * h
            hs[c, j] = h
            return carry

        lax.fori_loop(0, SUB, maps, 0)

        def tick(n, carry):
            j = n - WAVE * pos

            @pl.when((j >= 0) & (j < SUB))
            def _():
                @pl.when(pos > 0)
                def _():
                    upward(c, j).wait_recv()

                @pl.when(pos < chain - 1)
                def _():
                    gs[c, j] = gs[c, j] + sig[c, j] * gr[c, j]
                    upward(c, j).start()

            i = n - WAVE * (chain - 1 - pos)

            @pl.when((i >= 0) & (i < SUB))
            def _():
                @pl.when(pos < chain - 1)
                def _():
                    downward(c, i).wait_recv()

                @pl.when(pos > 0)
                def _():
                    hs[c, i] = hs[c, i] + rho[c, i] * hr[c, i]
                    downward(c, i).start()

            return carry

        lax.fori_loop(0, WAVE * (chain - 1) + SUB, tick, 0)

        def finish(j, carry):
            own = pl.ds(pl.multiple_of(j * nx, nx), nx)
            g = gr[c, j]
            for t in range(rows):
                g = modal[t, own] * rd[c, t, own] + w[c, t, own] * g
                modal[t, own] = g
            value = None
            for t in range(rows - 1, -1, -1):
                if value is None:
                    value = (g - e[c, t, own] * hr[c, j]) * last[c, j]
                else:
                    value = modal[t, own] - e[c, t, own] * value
                back = left(xb[...], value)
                at = pl.ds(pl.multiple_of((j * rows + t) * block, block), block)
                for q in range(cols):
                    bsend[q, c, at] = back[q * block : (q + 1) * block]
            for d in range(1, cols):
                back_copy(c, j, d, False).start()
            back_own(c, j).start()
            return carry

        lax.fori_loop(0, SUB, finish, 0)
        return carry

    lax.fori_loop(0, chunks, chunk, 0)

    def zstage(n, carry):
        c, j = n // SUB, lax.rem(n, SUB)
        back_own(c, j).wait()
        for d in range(1, cols):
            back_copy(c, j, d, True).wait_recv()
        part = pl.ds(pl.multiple_of(j * rows * block, rows * block), rows * block)
        for q in range(cols):
            brecv[q, c, part] = right(brecv[q, c, part], zb1[...], zb2[...])
        return carry

    lax.fori_loop(0, span, zstage, 0)

    def store(t):
        return pltpu.make_async_copy(field.at[t], out_ref.at[t], out_sem.at[t])

    def ystage(t, carry):
        for a in range(block):
            value = jnp.concatenate(
                [
                    brecv[q, c, pl.ds(t * block + a, SUB, stride=rows * block), :]
                    for q in range(cols)
                    for c in range(chunks)
                ],
                axis=0,
            )
            field[t, a] = left(yb[...], value)
        store(t).start()
        return carry

    lax.fori_loop(0, rows, ystage, 0)

    for c in range(chunks):
        for g in range(rows // group):
            for d in range(1, cols):
                forward_copy(c, g, d, False).wait_send()

    def drain(n, carry):
        c, j = n // SUB, lax.rem(n, SUB)
        for d in range(1, cols):
            back_copy(c, j, d, False).wait_send()

        @pl.when(pos < chain - 1)
        def _():
            upward(c, j).wait_send()

        @pl.when(pos > 0)
        def _():
            downward(c, j).wait_send()

        return carry

    lax.fori_loop(0, span, drain, 0)
    for t in range(rows):
        store(t).wait()


def parts(matrix):
    high = lax.reduce_precision(matrix, 8, 7)
    return high.astype(BF), (matrix - high).astype(BF)


def tripled(matrix):
    high, low = parts(matrix)
    return jnp.concatenate([high, high, low], axis=1)


def doubled(matrix):
    high, low = parts(matrix)
    return jnp.concatenate([high, high], axis=0), low


def local(chain, cols, right_side, basis_x, basis_y, basis_z, eig_x, eig_y, eig_z, steps):
    rows, block, ny, nz = right_side.shape
    nx = basis_x.shape[0]
    total = steps.shape[0]
    chunks = ny // cols // SUB
    group = 2 if rows % 2 == 0 else 1
    lengths = jnp.concatenate([steps / total, jnp.zeros((1,), steps.dtype)])
    mains = (lengths[:-1] + lengths[1:]) / 3.0
    sixth = lengths / 6.0
    closing = jnp.where(jnp.arange(total) == total - 1, 0.5, 0.0).astype(F32)
    vmem, smem, anywhere = (
        pl.BlockSpec(memory_space=pltpu.VMEM),
        pl.BlockSpec(memory_space=pltpu.SMEM),
        pl.BlockSpec(memory_space=pl.ANY),
    )
    modes = SUB * nx
    dma = pltpu.SemaphoreType.DMA
    table = pltpu.VMEM((chunks, rows, modes, nz), F32)
    tile = pltpu.VMEM((chunks, SUB, nx, nz), F32)
    travel = pltpu.VMEM((cols, chunks, rows, SUB * block, nz), F32)
    back = pltpu.VMEM((cols, chunks, SUB * rows * block, nz), F32)
    groups = rows // group
    return pl.pallas_call(
        partial(kernel, chain, cols, chunks, group),
        out_shape=jax.ShapeDtypeStruct(right_side.shape, F32),
        in_specs=[anywhere] + [vmem] * 9 + [smem] * 5,
        out_specs=anywhere,
        scratch_shapes=[
            pltpu.VMEM((rows, block, ny, nz), F32), travel, travel, pltpu.VMEM((rows, modes, nz), F32),
            table, table, table, table, table, tile, tile, tile, tile, tile, tile, tile, back, back,
            dma((rows,)), dma((rows,)),
            dma((chunks, groups, cols - 1)), dma((chunks, groups, cols - 1)), dma((chunks, groups)),
            dma((chunks, SUB, cols - 1)), dma((chunks, SUB, cols - 1)), dma((chunks, SUB)),
            dma((chunks, SUB)), dma((chunks, SUB)), dma((chunks, SUB)), dma((chunks, SUB)),
        ],
        compiler_params=pltpu.CompilerParams(
            collective_id=0, has_side_effects=True, vmem_limit_bytes=60 * 1024 * 1024
        ),
    )(
        right_side, *doubled(basis_z), *doubled(basis_z.T), tripled(basis_y.T), tripled(basis_y),
        tripled(basis_x.T), tripled(basis_x), eig_x[:, None] + eig_z[None, :],
        eig_y, mains, sixth, jnp.square(sixth), closing,
    )


def solution(mesh):
    return jax.shard_map(
        partial(local, mesh.shape["ta"], mesh.shape["gx"]),
        mesh=mesh,
        in_specs=(P("ta", "gx", None, None), P(), P(), P(), P(), P(), P(), P()),
        out_specs=P("ta", "gx", None, None),
        check_vma=False,
    )
```

```python
from functools import partial

import jax
import jax.numpy as jnp
from jax import lax
from jax.experimental import pallas as pl
from jax.experimental.pallas import tpu as pltpu
from jax.sharding import PartitionSpec as P

MESH = pl.DeviceIdType.MESH
SUB = 8
WAVE = 3
BF = jnp.bfloat16
F32 = jnp.float32


def halves(value):
    high = value.astype(BF)
    low = (value - high.astype(F32)).astype(BF)
    return high, low


def dot(a, b):
    return jnp.dot(a, b, preferred_element_type=F32)


def left(matrix, value):
    high, low = halves(value)
    return dot(matrix, jnp.concatenate([high, low, high], axis=0))


def right(value, twice, rest):
    high, low = halves(value)
    return dot(jnp.concatenate([high, low], axis=1), twice) + dot(high, rest)


def tripled(matrix):
    high, low = halves(matrix)
    return jnp.concatenate([high, high, low], axis=1)


def doubled(matrix):
    high, low = halves(matrix)
    return jnp.concatenate([high, high], axis=0), low


def kernel(
    chain, cols, chunks, group,
    x_ref, basis_x, basis_y, basis_z, eig_x, eig_z, eig_y, steps,
    out_ref,
    zf1, zf2, zb1, zb2, yf, yb, xf, xb, exz, mains, sixth, square,
    field, fsend, frecv, modal, rd, w, e, rdb, wb, last, sig, rho, gs, gr, hs, hr, bsend, brecv,
    in_sem, out_sem, fs_sem, fr_sem, fl_sem, bs_sem, br_sem, bl_sem, gs_sem, gr_sem, hs_sem, hr_sem,
):
    pos, me = lax.axis_index("ta"), lax.axis_index("gx")
    rows, block, ny, nz = field.shape
    nx, total = exz.shape[0], chain * rows
    span = chunks * SUB
    up, down = lax.rem(pos + 1, chain), lax.rem(pos + chain - 1, chain)

    def load(t):
        return pltpu.make_async_copy(x_ref.at[t], field.at[t], in_sem.at[t])

    for t in range(rows):
        load(t).start()

    barrier = pltpu.get_barrier_semaphore()
    for d in range(1, cols):
        pl.semaphore_signal(barrier, inc=1, device_id={"gx": lax.rem(me + d, cols)}, device_id_type=MESH)
    for other in (up, down):
        pl.semaphore_signal(barrier, inc=1, device_id={"ta": other}, device_id_type=MESH)
    pl.semaphore_wait(barrier, cols + 1)

    zf1[...], zf2[...] = doubled(basis_z[...])
    zb1[...], zb2[...] = doubled(basis_z[...].T)
    yf[...], yb[...] = tripled(basis_y[...].T), tripled(basis_y[...])
    xf[...], xb[...] = tripled(basis_x[...].T), tripled(basis_x[...])
    diagonal = lax.broadcasted_iota(jnp.int32, (nx, nx), 0) == lax.broadcasted_iota(jnp.int32, (nx, nx), 1)
    exz[...] = jnp.sum(jnp.where(diagonal, eig_x[...], 0.0), axis=1, keepdims=True) + eig_z[...]

    def lengths(k, carry):
        here = steps[k] * (1.0 / (6 * total))
        after = jnp.where(k + 1 < total, steps[jnp.minimum(k + 1, total - 1)], 0.0) * (1.0 / (6 * total))
        mains[k] = 2.0 * (here + after)
        sixth[k] = here
        square[k] = here * here
        return carry

    lax.fori_loop(0, total, lengths, 0)
    sixth[total] = 0.0
    square[total] = 0.0

    def closing(k):
        return jnp.where(k == total - 1, 0.5, 0.0)

    def forward_copy(c, g, d, receive):
        times = pl.ds(g * group, group)
        to, here = lax.rem(me + d, cols), me
        if receive:
            to, here = me, lax.rem(me + cols - d, cols)
        return pltpu.make_async_remote_copy(
            src_ref=fsend.at[to, c, times], dst_ref=frecv.at[here, c, times],
            send_sem=fs_sem.at[c, g, d - 1], recv_sem=fr_sem.at[c, g, d - 1],
            device_id={"gx": lax.rem(me + d, cols)}, device_id_type=MESH,
        )

    def forward_own(c, g):
        times = pl.ds(g * group, group)
        return pltpu.make_async_copy(fsend.at[me, c, times], frecv.at[me, c, times], fl_sem.at[c, g])

    def start_forward(c, g):
        for d in range(1, cols):
            forward_copy(c, g, d, False).start()
        forward_own(c, g).start()

    def transform(g, carry):
        for k in range(group):
            t = g * group + k
            load(t).wait()
            for first in range(0, block, 4):
                value = field[t, first : first + 4].reshape(4 * ny, nz)
                value = right(value, zf1[...], zf2[...])
                for a in range(4):
                    y = left(yf[...], value[a * ny : (a + 1) * ny])
                    for q in range(cols):
                        for c in range(chunks):
                            at = (q * chunks + c) * SUB
                            fsend[q, c, t, pl.ds(first + a, SUB, stride=block), :] = y[at : at + SUB]
        start_forward(0, g)
        return carry

    lax.fori_loop(0, rows // group, transform, 0)
    for c in range(1, chunks):
        for g in range(rows // group):
            start_forward(c, g)

    def shift_of(c, j):
        return exz[...] + eig_y[me * span + c * SUB + j]

    def matrices(n, carry):
        c, j = n // SUB, lax.rem(n, SUB)
        s = shift_of(c, j)
        s2 = s * s
        own = pl.ds(pl.multiple_of(j * nx, nx), nx)

        def coupling(k):
            return s2 * square[k] - 0.25

        def before(q, ratio):
            one, two = jnp.ones_like(s), ratio
            for r in range(rows):
                k = q * rows + r
                one, two = (s * mains[k]) * one - coupling(k) * two, one
            return two / one

        def after(n, ratio):
            q = chain - 1 - n
            one, two = jnp.ones_like(s), ratio
            for r in range(rows - 1, -1, -1):
                k = q * rows + r
                one, two = (s * mains[k] + closing(k)) * one - coupling(k + 1) * two, one
            return two / one

        ratio = lax.fori_loop(0, pos, before, jnp.zeros_like(s))
        product = None
        for r in range(rows):
            k = pos * rows + r
            ratio = 1.0 / (s * mains[k] + closing(k) - coupling(k) * ratio)
            rd[c, r, own] = ratio
            weight = (0.5 - s * sixth[k]) * ratio
            w[c, r, own] = weight
            product = weight if product is None else product * weight
            carry_over = (s * sixth[k + 1] + 0.5) * ratio
            e[c, r, own] = carry_over
        sig[c, j] = product
        ratio = lax.fori_loop(0, chain - 1 - pos, after, jnp.zeros_like(s))
        end = pos * rows + rows
        last[c, j] = 1.0 / (1.0 - carry_over * ((s * sixth[end] - 0.5) * ratio))
        product = None
        for r in range(rows - 1, -1, -1):
            k = pos * rows + r
            ratio = 1.0 / (s * mains[k] + closing(k) - coupling(k + 1) * ratio)
            rdb[c, r, own] = ratio
            weight = -(s * sixth[k + 1] + 0.5) * ratio
            wb[c, r, own] = weight
            product = weight if product is None else product * weight
        rho[c, j] = product
        return carry

    lax.fori_loop(0, span, matrices, 0)

    def chain_copy(send, receive, s_sem, r_sem, c, j, other):
        return pltpu.make_async_remote_copy(
            src_ref=send.at[c, j], dst_ref=receive.at[c, j], send_sem=s_sem.at[c, j], recv_sem=r_sem.at[c, j],
            device_id={"ta": other}, device_id_type=MESH,
        )

    def upward(c, j):
        return chain_copy(gs, gr, gs_sem, gr_sem, c, j, up)

    def downward(c, j):
        return chain_copy(hs, hr, hs_sem, hr_sem, c, j, down)

    first, final = pos == 0, pos == chain - 1

    @pl.when(first)
    def _():
        gr[...] = jnp.zeros_like(gr)

    @pl.when(final)
    def _():
        hr[...] = jnp.zeros_like(hr)

    def back_copy(c, j, d, receive):
        to, here = lax.rem(me + d, cols), me
        if receive:
            to, here = me, lax.rem(me + cols - d, cols)
        part = pl.ds(pl.multiple_of(j * rows * block, rows * block), rows * block)
        return pltpu.make_async_remote_copy(
            src_ref=bsend.at[to, c, part], dst_ref=brecv.at[here, c, part],
            send_sem=bs_sem.at[c, j, d - 1], recv_sem=br_sem.at[c, j, d - 1],
            device_id={"gx": lax.rem(me + d, cols)}, device_id_type=MESH,
        )

    def back_own(c, j):
        part = pl.ds(pl.multiple_of(j * rows * block, rows * block), rows * block)
        return pltpu.make_async_copy(bsend.at[me, c, part], brecv.at[me, c, part], bl_sem.at[c, j])

    def chunk(c, carry):
        def arrive(g, carry):
            forward_own(c, g).wait()
            for d in range(1, cols):
                forward_copy(c, g, d, True).wait_recv()
            for k in range(group):
                t = g * group + k
                for j in range(SUB):
                    value = jnp.concatenate(
                        [frecv[q, c, t, j * block : (j + 1) * block, :] for q in range(cols)], axis=0
                    )
                    modal[t, j * nx : (j + 1) * nx] = left(xf[...], value)
            return carry

        lax.fori_loop(0, rows // group, arrive, 0)

        def maps(j, carry):
            own = pl.ds(pl.multiple_of(j * nx, nx), nx)
            g = modal[0, own] * rd[c, 0, own]
            for t in range(1, rows):
                g = modal[t, own] * rd[c, t, own] + w[c, t, own] * g
            gs[c, j] = g
            h = modal[rows - 1, own] * rdb[c, rows - 1, own]
            for t in range(rows - 2, -1, -1):
                h = modal[t, own] * rdb[c, t, own] + wb[c, t, own] * h
            hs[c, j] = h
            return carry

        lax.fori_loop(0, SUB, maps, 0)

        def tick(n, carry):
            j = n - WAVE * pos

            @pl.when((j >= 0) & (j < SUB))
            def _():
                @pl.when(pos > 0)
                def _():
                    upward(c, j).wait_recv()

                @pl.when(pos < chain - 1)
                def _():
                    gs[c, j] = gs[c, j] + sig[c, j] * gr[c, j]
                    upward(c, j).start()

            i = n - WAVE * (chain - 1 - pos)

            @pl.when((i >= 0) & (i < SUB))
            def _():
                @pl.when(pos < chain - 1)
                def _():
                    downward(c, i).wait_recv()

                @pl.when(pos > 0)
                def _():
                    hs[c, i] = hs[c, i] + rho[c, i] * hr[c, i]
                    downward(c, i).start()

            return carry

        lax.fori_loop(0, WAVE * (chain - 1) + SUB, tick, 0)

        def finish(j, carry):
            own = pl.ds(pl.multiple_of(j * nx, nx), nx)
            g = gr[c, j]
            for t in range(rows):
                g = modal[t, own] * rd[c, t, own] + w[c, t, own] * g
                modal[t, own] = g
            value = None
            for t in range(rows - 1, -1, -1):
                if value is None:
                    value = (g - e[c, t, own] * hr[c, j]) * last[c, j]
                else:
                    value = modal[t, own] - e[c, t, own] * value
                back = left(xb[...], value)
                at = pl.ds(pl.multiple_of((j * rows + t) * block, block), block)
                for q in range(cols):
                    bsend[q, c, at] = back[q * block : (q + 1) * block]
            for d in range(1, cols):
                back_copy(c, j, d, False).start()
            back_own(c, j).start()
            return carry

        lax.fori_loop(0, SUB, finish, 0)
        return carry

    lax.fori_loop(0, chunks, chunk, 0)

    def zstage(n, carry):
        c, j = n // SUB, lax.rem(n, SUB)
        back_own(c, j).wait()
        for d in range(1, cols):
            back_copy(c, j, d, True).wait_recv()
        part = pl.ds(pl.multiple_of(j * rows * block, rows * block), rows * block)
        for q in range(cols):
            brecv[q, c, part] = right(brecv[q, c, part], zb1[...], zb2[...])
        return carry

    lax.fori_loop(0, span, zstage, 0)

    def store(t):
        return pltpu.make_async_copy(field.at[t], out_ref.at[t], out_sem.at[t])

    def ystage(t, carry):
        for a in range(block):
            value = jnp.concatenate(
                [
                    brecv[q, c, pl.ds(t * block + a, SUB, stride=rows * block), :]
                    for q in range(cols)
                    for c in range(chunks)
                ],
                axis=0,
            )
            field[t, a] = left(yb[...], value)
        store(t).start()
        return carry

    lax.fori_loop(0, rows, ystage, 0)

    for c in range(chunks):
        for g in range(rows // group):
            for d in range(1, cols):
                forward_copy(c, g, d, False).wait_send()

    def drain(n, carry):
        c, j = n // SUB, lax.rem(n, SUB)
        for d in range(1, cols):
            back_copy(c, j, d, False).wait_send()

        @pl.when(pos < chain - 1)
        def _():
            upward(c, j).wait_send()

        @pl.when(pos > 0)
        def _():
            downward(c, j).wait_send()

        return carry

    lax.fori_loop(0, span, drain, 0)
    for t in range(rows):
        store(t).wait()


def local(chain, cols, right_side, basis_x, basis_y, basis_z, eig_x, eig_y, eig_z, steps):
    rows, block, ny, nz = right_side.shape
    nx = basis_x.shape[0]
    total = steps.shape[0]
    chunks = ny // cols // SUB
    group = 2 if rows % 2 == 0 else 1
    vmem, smem, anywhere = (
        pl.BlockSpec(memory_space=pltpu.VMEM),
        pl.BlockSpec(memory_space=pltpu.SMEM),
        pl.BlockSpec(memory_space=pl.ANY),
    )
    modes = SUB * nx
    dma = pltpu.SemaphoreType.DMA
    table = pltpu.VMEM((chunks, rows, modes, nz), F32)
    tile = pltpu.VMEM((chunks, SUB, nx, nz), F32)
    travel = pltpu.VMEM((cols, chunks, rows, SUB * block, nz), F32)
    back = pltpu.VMEM((cols, chunks, SUB * rows * block, nz), F32)
    groups = rows // group
    return pl.pallas_call(
        partial(kernel, chain, cols, chunks, group),
        out_shape=jax.ShapeDtypeStruct(right_side.shape, F32),
        in_specs=[anywhere] + [vmem] * 5 + [smem] * 2,
        out_specs=anywhere,
        scratch_shapes=[
            pltpu.VMEM((2 * nz, nz), BF), pltpu.VMEM((nz, nz), BF), pltpu.VMEM((2 * nz, nz), BF), pltpu.VMEM((nz, nz), BF),
            pltpu.VMEM((ny, 3 * ny), BF), pltpu.VMEM((ny, 3 * ny), BF),
            pltpu.VMEM((nx, 3 * nx), BF), pltpu.VMEM((nx, 3 * nx), BF), pltpu.VMEM((nx, nz), F32),
            pltpu.SMEM((total,), F32), pltpu.SMEM((total + 1,), F32), pltpu.SMEM((total + 1,), F32),
            pltpu.VMEM((rows, block, ny, nz), F32), travel, travel, pltpu.VMEM((rows, modes, nz), F32),
            table, table, table, table, table, tile, tile, tile, tile, tile, tile, tile, back, back,
            dma((rows,)), dma((rows,)),
            dma((chunks, groups, cols - 1)), dma((chunks, groups, cols - 1)), dma((chunks, groups)),
            dma((chunks, SUB, cols - 1)), dma((chunks, SUB, cols - 1)), dma((chunks, SUB)),
            dma((chunks, SUB)), dma((chunks, SUB)), dma((chunks, SUB)), dma((chunks, SUB)),
        ],
        compiler_params=pltpu.CompilerParams(
            collective_id=0, has_side_effects=True, vmem_limit_bytes=60 * 1024 * 1024
        ),
    )(
        right_side, basis_x, basis_y, basis_z, eig_x.reshape(1, nx), eig_z.reshape(1, nz), eig_y, steps
    )


def solution(mesh):
    return jax.shard_map(
        partial(local, mesh.shape["ta"], mesh.shape["gx"]),
        mesh=mesh,
        in_specs=(P("ta", "gx", None, None), P(), P(), P(), P(), P(), P(), P()),
        out_specs=P("ta", "gx", None, None),
        check_vma=False,
    )
```

```python
from functools import partial

import jax
import jax.numpy as jnp
from jax import lax
from jax.experimental import pallas as pl
from jax.experimental.pallas import tpu as pltpu
from jax.sharding import PartitionSpec as P

MESH = pl.DeviceIdType.MESH
SUB = 8
WAVE = 2
BF = jnp.bfloat16
F32 = jnp.float32


def halves(value):
    high = value.astype(BF)
    low = (value - high.astype(F32)).astype(BF)
    return high, low


def dot(a, b):
    return jnp.dot(a, b, preferred_element_type=F32)


def left(matrix, value):
    high, low = halves(value)
    return dot(matrix, jnp.concatenate([high, low, high], axis=0))


def left_pair(matrix, one, two):
    both = left(matrix, jnp.concatenate([one, two], axis=1))
    width = one.shape[1]
    return both[:, :width], both[:, width:]


def right(value, twice, rest):
    high, low = halves(value)
    return dot(jnp.concatenate([high, low], axis=1), twice) + dot(high, rest)


def tripled(matrix):
    high, low = halves(matrix)
    return jnp.concatenate([high, high, low], axis=1)


def doubled(matrix):
    high, low = halves(matrix)
    return jnp.concatenate([high, high], axis=0), low


def kernel(
    chain, cols, chunks, group,
    x_ref, basis_x, basis_y, basis_z, eig_x, eig_z, eig_y, steps,
    out_ref,
    zf1, zf2, zb1, zb2, yf, yb, xf, xb, exz, mains, sixth, square,
    field, fsend, frecv, modal, rd, w, e, rdb, wb, last, steps_own, steps_other, maps_own, maps_other, gs, gr, hs, hr, gin, hin,
    bsend, brecv,
    in_sem, out_sem, fs_sem, fr_sem, fl_sem, bs_sem, br_sem, bl_sem, gs_sem, gr_sem, hs_sem, hr_sem,
    ms_sem, mr_sem,
):
    pos, me = lax.axis_index("ta"), lax.axis_index("gx")
    rows, block, ny, nz = field.shape
    nx, total = exz.shape[0], chain * rows
    span = chunks * SUB
    level, side, levels = pos // 2, lax.rem(pos, 2), chain // 2
    partner = pos + 1 - 2 * side
    up, down = lax.rem(pos + 2, chain), lax.rem(pos + chain - 2, chain)

    def load(t):
        return pltpu.make_async_copy(x_ref.at[t], field.at[t], in_sem.at[t])

    for t in range(rows):
        load(t).start()

    barrier = pltpu.get_barrier_semaphore()
    for d in range(1, cols):
        pl.semaphore_signal(barrier, inc=1, device_id={"gx": lax.rem(me + d, cols)}, device_id_type=MESH)
    for other in (partner, up, down):
        pl.semaphore_signal(barrier, inc=1, device_id={"ta": other}, device_id_type=MESH)
    pl.semaphore_wait(barrier, cols + 2)

    zf1[...], zf2[...] = doubled(basis_z[...])
    zb1[...], zb2[...] = doubled(basis_z[...].T)
    yf[...], yb[...] = tripled(basis_y[...].T), tripled(basis_y[...])
    xf[...], xb[...] = tripled(basis_x[...].T), tripled(basis_x[...])
    diagonal = lax.broadcasted_iota(jnp.int32, (nx, nx), 0) == lax.broadcasted_iota(jnp.int32, (nx, nx), 1)
    exz[...] = jnp.sum(jnp.where(diagonal, eig_x[...], 0.0), axis=1, keepdims=True) + eig_z[...]

    def lengths(k, carry):
        here = steps[k] * (1.0 / (6 * total))
        after = jnp.where(k + 1 < total, steps[jnp.minimum(k + 1, total - 1)], 0.0) * (1.0 / (6 * total))
        mains[k] = 2.0 * (here + after)
        sixth[k] = here
        square[k] = here * here
        return carry

    lax.fori_loop(0, total, lengths, 0)
    sixth[total] = 0.0
    square[total] = 0.0

    def closing(k):
        return jnp.where(k == total - 1, 0.5, 0.0)

    def forward_copy(c, g, d, receive):
        times = pl.ds(g * group, group)
        to, here = lax.rem(me + d, cols), me
        if receive:
            to, here = me, lax.rem(me + cols - d, cols)
        return pltpu.make_async_remote_copy(
            src_ref=fsend.at[to, c, times], dst_ref=frecv.at[here, c, times],
            send_sem=fs_sem.at[c, g, d - 1], recv_sem=fr_sem.at[c, g, d - 1],
            device_id={"gx": lax.rem(me + d, cols)}, device_id_type=MESH,
        )

    def forward_own(c, g):
        times = pl.ds(g * group, group)
        return pltpu.make_async_copy(fsend.at[me, c, times], frecv.at[me, c, times], fl_sem.at[c, g])

    def start_forward(c, g):
        for d in range(1, cols):
            forward_copy(c, g, d, False).start()
        forward_own(c, g).start()

    def transform(g, carry):
        for k in range(group):
            t = g * group + k
            load(t).wait()
            for first in range(0, block, 4):
                value = field[t, first : first + 4].reshape(4 * ny, nz)
                value = right(value, zf1[...], zf2[...])
                for a in range(0, 4, 2):
                    pair = left_pair(
                        yf[...], value[a * ny : (a + 1) * ny], value[(a + 1) * ny : (a + 2) * ny]
                    )
                    for k2, y in enumerate(pair):
                        for q in range(cols):
                            for c in range(chunks):
                                at = (q * chunks + c) * SUB
                                fsend[q, c, t, pl.ds(first + a + k2, SUB, stride=block), :] = y[at : at + SUB]
        start_forward(0, g)
        return carry

    lax.fori_loop(0, rows // group, transform, 0)
    for c in range(1, chunks):
        for g in range(rows // group):
            start_forward(c, g)

    def shift_of(c, j):
        return exz[...] + eig_y[me * span + c * SUB + j]

    def matrices(n, carry):
        c, j = n // SUB, lax.rem(n, SUB)
        s = shift_of(c, j)
        s2 = s * s
        own = pl.ds(pl.multiple_of(j * nx, nx), nx)

        def coupling(k):
            return s2 * square[k] - 0.25

        def before(q, state):
            one, two = jnp.ones_like(s), state[0]
            product = one
            for r in range(rows):
                k = q * rows + r
                one, two = (s * mains[k] + closing(k)) * one - coupling(k) * two, one
                product = product * (0.5 - s * sixth[k])
            return two / one, product / one

        def after(q, state):
            one, two = jnp.ones_like(s), state[0]
            product = one
            for r in range(rows - 1, -1, -1):
                k = q * rows + r
                one, two = (s * mains[k] + closing(k)) * one - coupling(k + 1) * two, one
                product = product * -(s * sixth[k + 1] + 0.5)
            return two / one, product / one

        start = (jnp.zeros_like(s), jnp.ones_like(s))
        ratio, passed = lax.fori_loop(0, pos, before, start)
        product = None
        for r in range(rows):
            k = pos * rows + r
            ratio = 1.0 / (s * mains[k] + closing(k) - coupling(k) * ratio)
            rd[c, r, own] = ratio
            weight = (0.5 - s * sixth[k]) * ratio
            w[c, r, own] = weight
            product = weight if product is None else product * weight
            carry_over = (s * sixth[k + 1] + 0.5) * ratio
            e[c, r, own] = carry_over
        steps_own[c, j, 0] = product
        steps_other[c, j, 0] = lax.fori_loop(
            0, 1 - side, lambda n, state: before(pos + 1, state), (ratio, passed)
        )[1]
        ratio, passed = lax.fori_loop(
            0, chain - 1 - pos, lambda n, state: after(chain - 1 - n, state), start
        )
        end = pos * rows + rows
        last[c, j] = 1.0 / (1.0 - carry_over * ((s * sixth[end] - 0.5) * ratio))
        product = None
        for r in range(rows - 1, -1, -1):
            k = pos * rows + r
            ratio = 1.0 / (s * mains[k] + closing(k) - coupling(k + 1) * ratio)
            rdb[c, r, own] = ratio
            weight = -(s * sixth[k + 1] + 0.5) * ratio
            wb[c, r, own] = weight
            product = weight if product is None else product * weight
        steps_own[c, j, 1] = product
        steps_other[c, j, 1] = lax.fori_loop(
            0, side, lambda n, state: after(pos - 1, state), (ratio, passed)
        )[1]
        return carry

    lax.fori_loop(0, span, matrices, 0)

    def maps_copy(c, j):
        return pltpu.make_async_remote_copy(
            src_ref=maps_own.at[c, j], dst_ref=maps_other.at[c, j],
            send_sem=ms_sem.at[c, j], recv_sem=mr_sem.at[c, j],
            device_id={"ta": partner}, device_id_type=MESH,
        )


    def chain_copy(send, receive, s_sem, r_sem, c, j, other):
        return pltpu.make_async_remote_copy(
            src_ref=send.at[c, j], dst_ref=receive.at[c, j], send_sem=s_sem.at[c, j], recv_sem=r_sem.at[c, j],
            device_id={"ta": other}, device_id_type=MESH,
        )

    def upward(c, j):
        return chain_copy(gs, gr, gs_sem, gr_sem, c, j, up)

    def downward(c, j):
        return chain_copy(hs, hr, hs_sem, hr_sem, c, j, down)

    first, final = level == 0, level == levels - 1

    @pl.when(first)
    def _():
        gr[...] = jnp.zeros_like(gr)

    @pl.when(final)
    def _():
        hr[...] = jnp.zeros_like(hr)

    def back_copy(c, j, d, receive):
        to, here = lax.rem(me + d, cols), me
        if receive:
            to, here = me, lax.rem(me + cols - d, cols)
        part = pl.ds(pl.multiple_of(j * rows * block, rows * block), rows * block)
        return pltpu.make_async_remote_copy(
            src_ref=bsend.at[to, c, part], dst_ref=brecv.at[here, c, part],
            send_sem=bs_sem.at[c, j, d - 1], recv_sem=br_sem.at[c, j, d - 1],
            device_id={"gx": lax.rem(me + d, cols)}, device_id_type=MESH,
        )

    def back_own(c, j):
        part = pl.ds(pl.multiple_of(j * rows * block, rows * block), rows * block)
        return pltpu.make_async_copy(bsend.at[me, c, part], brecv.at[me, c, part], bl_sem.at[c, j])

    def chunk(c, carry):
        def arrive(g, carry):
            forward_own(c, g).wait()
            for d in range(1, cols):
                forward_copy(c, g, d, True).wait_recv()
            for k in range(group):
                t = g * group + k
                for j in range(0, SUB, 2):
                    pair = left_pair(xf[...], *(
                        jnp.concatenate([frecv[q, c, t, i * block : (i + 1) * block, :] for q in range(cols)], axis=0)
                        for i in (j, j + 1)
                    ))
                    for k2, value in enumerate(pair):
                        modal[t, (j + k2) * nx : (j + k2 + 1) * nx] = value
            return carry

        lax.fori_loop(0, rows // group, arrive, 0)

        def maps(j, carry):
            own = pl.ds(pl.multiple_of(j * nx, nx), nx)
            g = modal[0, own] * rd[c, 0, own]
            for t in range(1, rows):
                g = modal[t, own] * rd[c, t, own] + w[c, t, own] * g
            maps_own[c, j, 0] = g
            h = modal[rows - 1, own] * rdb[c, rows - 1, own]
            for t in range(rows - 2, -1, -1):
                h = modal[t, own] * rdb[c, t, own] + wb[c, t, own] * h
            maps_own[c, j, 1] = h
            maps_copy(c, j).start()
            return carry

        lax.fori_loop(0, SUB, maps, 0)

        def finish(j):
            own = pl.ds(pl.multiple_of(j * nx, nx), nx)
            g = jnp.where(side == 0, gr[c, j], gin[c, j])
            later = jnp.where(side == 1, hr[c, j], hin[c, j])
            for t in range(rows):
                g = modal[t, own] * rd[c, t, own] + w[c, t, own] * g
                modal[t, own] = g
            value, waiting = None, []
            for t in range(rows - 1, -1, -1):
                if value is None:
                    value = (g - e[c, t, own] * later) * last[c, j]
                else:
                    value = modal[t, own] - e[c, t, own] * value
                waiting.append((t, value))
                if len(waiting) == 2 or t == 0:
                    if len(waiting) == 2:
                        done = left_pair(xb[...], waiting[0][1], waiting[1][1])
                    else:
                        done = (left(xb[...], value),)
                    for (t2, _), back in zip(waiting, done):
                        at = pl.ds(pl.multiple_of((j * rows + t2) * block, block), block)
                        for q in range(cols):
                            bsend[q, c, at] = back[q * block : (q + 1) * block]
                    waiting = []
            for d in range(1, cols):
                back_copy(c, j, d, False).start()
            back_own(c, j).start()

        def tick(n, carry):
            @pl.when(n < SUB)
            def _():
                maps_copy(c, n).wait_recv()

            j = n - WAVE * level

            @pl.when((j >= 0) & (j < SUB))
            def _():
                @pl.when(level > 0)
                def _():
                    upward(c, j).wait_recv()

                carried = gr[c, j]
                kept, passed = maps_own[c, j, 0], maps_other[c, j, 0]
                kept_step, passed_step = steps_own[c, j, 0], steps_other[c, j, 0]

                @pl.when(side == 0)
                def _():
                    gs[c, j] = passed + passed_step * (kept + kept_step * carried)

                @pl.when(side == 1)
                def _():
                    inner = passed + passed_step * carried
                    gin[c, j] = inner
                    gs[c, j] = kept + kept_step * inner

                @pl.when(level < levels - 1)
                def _():
                    upward(c, j).start()

            i = n - WAVE * (levels - 1 - level)

            @pl.when((i >= 0) & (i < SUB))
            def _():
                @pl.when(level < levels - 1)
                def _():
                    downward(c, i).wait_recv()

                carried = hr[c, i]
                kept, passed = maps_own[c, i, 1], maps_other[c, i, 1]
                kept_step, passed_step = steps_own[c, i, 1], steps_other[c, i, 1]

                @pl.when(side == 1)
                def _():
                    hs[c, i] = passed + passed_step * (kept + kept_step * carried)

                @pl.when(side == 0)
                def _():
                    inner = passed + passed_step * carried
                    hin[c, i] = inner
                    hs[c, i] = kept + kept_step * inner

                @pl.when(level > 0)
                def _():
                    downward(c, i).start()

            f = n - WAVE * jnp.maximum(level, levels - 1 - level)

            @pl.when((f >= 0) & (f < SUB))
            def _():
                finish(f)

            return carry

        lax.fori_loop(0, WAVE * (levels - 1) + SUB, tick, 0)

        return carry

    lax.fori_loop(0, chunks, chunk, 0)

    def zstage(n, carry):
        c, j = n // SUB, lax.rem(n, SUB)
        back_own(c, j).wait()
        for d in range(1, cols):
            back_copy(c, j, d, True).wait_recv()
        part = pl.ds(pl.multiple_of(j * rows * block, rows * block), rows * block)
        for q in range(cols):
            brecv[q, c, part] = right(brecv[q, c, part], zb1[...], zb2[...])
        return carry

    lax.fori_loop(0, span, zstage, 0)

    def store(t):
        return pltpu.make_async_copy(field.at[t], out_ref.at[t], out_sem.at[t])

    def ystage(t, carry):
        for a in range(0, block, 2):
            field[t, a], field[t, a + 1] = left_pair(yb[...], *(
                jnp.concatenate(
                    [
                        brecv[q, c, pl.ds(t * block + i, SUB, stride=rows * block), :]
                        for q in range(cols)
                        for c in range(chunks)
                    ],
                    axis=0,
                )
                for i in (a, a + 1)
            ))
        store(t).start()
        return carry

    lax.fori_loop(0, rows, ystage, 0)

    for c in range(chunks):
        for g in range(rows // group):
            for d in range(1, cols):
                forward_copy(c, g, d, False).wait_send()

    def drain(n, carry):
        c, j = n // SUB, lax.rem(n, SUB)
        for d in range(1, cols):
            back_copy(c, j, d, False).wait_send()

        maps_copy(c, j).wait_send()

        @pl.when(level < levels - 1)
        def _():
            upward(c, j).wait_send()

        @pl.when(level > 0)
        def _():
            downward(c, j).wait_send()

        return carry

    lax.fori_loop(0, span, drain, 0)
    for t in range(rows):
        store(t).wait()


def local(chain, cols, right_side, basis_x, basis_y, basis_z, eig_x, eig_y, eig_z, steps):
    rows, block, ny, nz = right_side.shape
    nx = basis_x.shape[0]
    total = steps.shape[0]
    chunks = ny // cols // SUB
    group = 2 if rows % 2 == 0 else 1
    vmem, smem, anywhere = (
        pl.BlockSpec(memory_space=pltpu.VMEM),
        pl.BlockSpec(memory_space=pltpu.SMEM),
        pl.BlockSpec(memory_space=pl.ANY),
    )
    modes = SUB * nx
    dma = pltpu.SemaphoreType.DMA
    table = pltpu.VMEM((chunks, rows, modes, nz), F32)
    tile = pltpu.VMEM((chunks, SUB, nx, nz), F32)
    twin = pltpu.VMEM((chunks, SUB, 2, nx, nz), F32)
    travel = pltpu.VMEM((cols, chunks, rows, SUB * block, nz), F32)
    back = pltpu.VMEM((cols, chunks, SUB * rows * block, nz), F32)
    groups = rows // group
    return pl.pallas_call(
        partial(kernel, chain, cols, chunks, group),
        out_shape=jax.ShapeDtypeStruct(right_side.shape, F32),
        in_specs=[anywhere] + [vmem] * 5 + [smem] * 2,
        out_specs=anywhere,
        scratch_shapes=[
            pltpu.VMEM((2 * nz, nz), BF), pltpu.VMEM((nz, nz), BF), pltpu.VMEM((2 * nz, nz), BF), pltpu.VMEM((nz, nz), BF),
            pltpu.VMEM((ny, 3 * ny), BF), pltpu.VMEM((ny, 3 * ny), BF),
            pltpu.VMEM((nx, 3 * nx), BF), pltpu.VMEM((nx, 3 * nx), BF), pltpu.VMEM((nx, nz), F32),
            pltpu.SMEM((total,), F32), pltpu.SMEM((total + 1,), F32), pltpu.SMEM((total + 1,), F32),
            pltpu.VMEM((rows, block, ny, nz), F32), travel, travel, pltpu.VMEM((rows, modes, nz), F32),
            table, table, table, table, table, tile, twin, twin, twin, twin,
            tile, tile, tile, tile, tile, tile, back, back,
            dma((rows,)), dma((rows,)),
            dma((chunks, groups, cols - 1)), dma((chunks, groups, cols - 1)), dma((chunks, groups)),
            dma((chunks, SUB, cols - 1)), dma((chunks, SUB, cols - 1)), dma((chunks, SUB)),
            dma((chunks, SUB)), dma((chunks, SUB)), dma((chunks, SUB)), dma((chunks, SUB)),
            dma((chunks, SUB)), dma((chunks, SUB)),
        ],
        compiler_params=pltpu.CompilerParams(
            collective_id=0, has_side_effects=True, vmem_limit_bytes=60 * 1024 * 1024
        ),
    )(
        right_side, basis_x, basis_y, basis_z, eig_x.reshape(1, nx), eig_z.reshape(1, nz), eig_y, steps
    )


def solution(mesh):
    return jax.shard_map(
        partial(local, mesh.shape["ta"], mesh.shape["gx"]),
        mesh=mesh,
        in_specs=(P("ta", "gx", None, None), P(), P(), P(), P(), P(), P(), P()),
        out_specs=P("ta", "gx", None, None),
        check_vma=False,
    )
```

```python
from functools import partial

import jax
import jax.numpy as jnp
from jax import lax
from jax.experimental import pallas as pl
from jax.experimental.pallas import tpu as pltpu
from jax.sharding import PartitionSpec as P

MESH = pl.DeviceIdType.MESH
SUB = 8
WAVE = 2
BF = jnp.bfloat16
F32 = jnp.float32


def halves(value):
    high = value.astype(BF)
    low = (value - high.astype(F32)).astype(BF)
    return high, low


def dot(a, b):
    return jnp.dot(a, b, preferred_element_type=F32)


def left(matrix, value):
    high, low = halves(value)
    return dot(matrix, jnp.concatenate([high, low, high], axis=0))


def left_pair(matrix, one, two):
    both = left(matrix, jnp.concatenate([one, two], axis=1))
    width = one.shape[1]
    return both[:, :width], both[:, width:]


def right(value, twice, rest):
    high, low = halves(value)
    return dot(jnp.concatenate([high, low], axis=1), twice) + dot(high, rest)


def tripled(matrix):
    high, low = halves(matrix)
    return jnp.concatenate([high, high, low], axis=1)


def doubled(matrix):
    high, low = halves(matrix)
    return jnp.concatenate([high, high], axis=0), low


def kernel(
    chain, cols, chunks, group,
    x_ref, basis_x, basis_y, basis_z, eig_x, eig_z, eig_y, steps,
    out_ref,
    zf1, zf2, zb1, zb2, yf, yb, xf, xb, exz, mains, sixth, square,
    field, fsend, frecv, modal, rd, w, e, rdb, wb, last, steps_own, steps_other, maps_own, maps_other, gs, gr, hs, hr, gin, hin,
    bsend, brecv,
    in_sem, out_sem, fs_sem, fr_sem, fl_sem, bs_sem, br_sem, bl_sem, gs_sem, gr_sem, hs_sem, hr_sem,
    ms_sem, mr_sem,
):
    pos, me = lax.axis_index("ta"), lax.axis_index("gx")
    rows, block, ny, nz = field.shape
    nx, total = exz.shape[0], chain * rows
    span = chunks * SUB
    level, side, levels = pos // 2, lax.rem(pos, 2), chain // 2
    partner = pos + 1 - 2 * side
    up, down = lax.rem(pos + 2, chain), lax.rem(pos + chain - 2, chain)

    def load(t):
        return pltpu.make_async_copy(x_ref.at[t], field.at[t], in_sem.at[t])

    for t in range(rows):
        load(t).start()

    barrier = pltpu.get_barrier_semaphore()
    for d in range(1, cols):
        pl.semaphore_signal(barrier, inc=1, device_id={"gx": lax.rem(me + d, cols)}, device_id_type=MESH)
    for other in (partner, up, down):
        pl.semaphore_signal(barrier, inc=1, device_id={"ta": other}, device_id_type=MESH)
    pl.semaphore_wait(barrier, cols + 2)

    zf1[...], zf2[...] = doubled(basis_z[...])
    zb1[...], zb2[...] = doubled(basis_z[...].T)
    yf[...], yb[...] = tripled(basis_y[...].T), tripled(basis_y[...])
    xf[...], xb[...] = tripled(basis_x[...].T), tripled(basis_x[...])
    diagonal = lax.broadcasted_iota(jnp.int32, (nx, nx), 0) == lax.broadcasted_iota(jnp.int32, (nx, nx), 1)
    exz[...] = jnp.sum(jnp.where(diagonal, eig_x[...], 0.0), axis=1, keepdims=True) + eig_z[...]

    def lengths(k, carry):
        here = steps[k] * (1.0 / (6 * total))
        after = jnp.where(k + 1 < total, steps[jnp.minimum(k + 1, total - 1)], 0.0) * (1.0 / (6 * total))
        mains[k] = 2.0 * (here + after)
        sixth[k] = here
        square[k] = here * here
        return carry

    lax.fori_loop(0, total, lengths, 0)
    sixth[total] = 0.0
    square[total] = 0.0

    def closing(k):
        return jnp.where(k == total - 1, 0.5, 0.0)

    def forward_copy(c, g, d, receive):
        times = pl.ds(g * group, group)
        to, here = lax.rem(me + d, cols), me
        if receive:
            to, here = me, lax.rem(me + cols - d, cols)
        return pltpu.make_async_remote_copy(
            src_ref=fsend.at[to, c, times], dst_ref=frecv.at[here, c, times],
            send_sem=fs_sem.at[c, g, d - 1], recv_sem=fr_sem.at[c, g, d - 1],
            device_id={"gx": lax.rem(me + d, cols)}, device_id_type=MESH,
        )

    def forward_own(c, g):
        times = pl.ds(g * group, group)
        return pltpu.make_async_copy(fsend.at[me, c, times], frecv.at[me, c, times], fl_sem.at[c, g])

    def start_forward(c, g):
        for d in range(1, cols):
            forward_copy(c, g, d, False).start()
        forward_own(c, g).start()

    def transform(g, carry):
        for k in range(group):
            t = g * group + k
            load(t).wait()
            for first in range(0, block, 4):
                value = field[t, first : first + 4].reshape(4 * ny, nz)
                value = right(value, zf1[...], zf2[...])
                for a in range(0, 4, 2):
                    pair = left_pair(
                        yf[...], value[a * ny : (a + 1) * ny], value[(a + 1) * ny : (a + 2) * ny]
                    )
                    for k2, y in enumerate(pair):
                        for q in range(cols):
                            for c in range(chunks):
                                at = (q * chunks + c) * SUB
                                fsend[q, c, t, pl.ds(first + a + k2, SUB, stride=block), :] = y[at : at + SUB]
        start_forward(0, g)
        return carry

    lax.fori_loop(0, rows // group, transform, 0)
    for c in range(1, chunks):
        for g in range(rows // group):
            start_forward(c, g)

    def shift_of(c, j):
        return exz[...] + eig_y[me * span + c * SUB + j]

    def matrices(n, carry):
        c, j = n // SUB, lax.rem(n, SUB)
        s = shift_of(c, j)
        s2 = s * s
        own = pl.ds(pl.multiple_of(j * nx, nx), nx)

        def coupling(k):
            return s2 * square[k] - 0.25

        def before(q, state):
            one, two = jnp.ones_like(s), state[0]
            product = one
            for r in range(rows):
                k = q * rows + r
                one, two = (s * mains[k] + closing(k)) * one - coupling(k) * two, one
                product = product * (0.5 - s * sixth[k])
            return two / one, product / one

        def after(q, state):
            one, two = jnp.ones_like(s), state[0]
            product = one
            for r in range(rows - 1, -1, -1):
                k = q * rows + r
                one, two = (s * mains[k] + closing(k)) * one - coupling(k + 1) * two, one
                product = product * -(s * sixth[k + 1] + 0.5)
            return two / one, product / one

        start = (jnp.zeros_like(s), jnp.ones_like(s))
        ratio, passed = lax.fori_loop(0, pos, before, start)
        product = None
        for r in range(rows):
            k = pos * rows + r
            ratio = 1.0 / (s * mains[k] + closing(k) - coupling(k) * ratio)
            rd[c, r, own] = ratio
            weight = (0.5 - s * sixth[k]) * ratio
            w[c, r, own] = weight
            product = weight if product is None else product * weight
            carry_over = (s * sixth[k + 1] + 0.5) * ratio
            e[c, r, own] = carry_over
        steps_own[c, j, 0] = product
        steps_other[c, j, 0] = lax.fori_loop(
            0, 1 - side, lambda n, state: before(pos + 1, state), (ratio, passed)
        )[1]
        ratio, passed = lax.fori_loop(
            0, chain - 1 - pos, lambda n, state: after(chain - 1 - n, state), start
        )
        end = pos * rows + rows
        last[c, j] = 1.0 / (1.0 - carry_over * ((s * sixth[end] - 0.5) * ratio))
        product = None
        for r in range(rows - 1, -1, -1):
            k = pos * rows + r
            ratio = 1.0 / (s * mains[k] + closing(k) - coupling(k + 1) * ratio)
            rdb[c, r, own] = ratio
            weight = -(s * sixth[k + 1] + 0.5) * ratio
            wb[c, r, own] = weight
            product = weight if product is None else product * weight
        steps_own[c, j, 1] = product
        steps_other[c, j, 1] = lax.fori_loop(
            0, side, lambda n, state: after(pos - 1, state), (ratio, passed)
        )[1]
        return carry

    lax.fori_loop(0, span, matrices, 0)

    def maps_copy(c, j):
        return pltpu.make_async_remote_copy(
            src_ref=maps_own.at[c, j], dst_ref=maps_other.at[c, j],
            send_sem=ms_sem.at[c, j], recv_sem=mr_sem.at[c, j],
            device_id={"ta": partner}, device_id_type=MESH,
        )


    def chain_copy(send, receive, s_sem, r_sem, c, j, other):
        return pltpu.make_async_remote_copy(
            src_ref=send.at[c, j], dst_ref=receive.at[c, j], send_sem=s_sem.at[c, j], recv_sem=r_sem.at[c, j],
            device_id={"ta": other}, device_id_type=MESH,
        )

    def upward(c, j):
        return chain_copy(gs, gr, gs_sem, gr_sem, c, j, up)

    def downward(c, j):
        return chain_copy(hs, hr, hs_sem, hr_sem, c, j, down)

    first, final = level == 0, level == levels - 1

    @pl.when(first)
    def _():
        gr[...] = jnp.zeros_like(gr)

    @pl.when(final)
    def _():
        hr[...] = jnp.zeros_like(hr)

    def back_copy(c, j, d, receive):
        to, here = lax.rem(me + d, cols), me
        if receive:
            to, here = me, lax.rem(me + cols - d, cols)
        part = pl.ds(pl.multiple_of(j * rows * block, rows * block), rows * block)
        return pltpu.make_async_remote_copy(
            src_ref=bsend.at[to, c, part], dst_ref=brecv.at[here, c, part],
            send_sem=bs_sem.at[c, j, d - 1], recv_sem=br_sem.at[c, j, d - 1],
            device_id={"gx": lax.rem(me + d, cols)}, device_id_type=MESH,
        )

    def back_own(c, j):
        part = pl.ds(pl.multiple_of(j * rows * block, rows * block), rows * block)
        return pltpu.make_async_copy(bsend.at[me, c, part], brecv.at[me, c, part], bl_sem.at[c, j])

    def chunk(c, carry):
        def arrive(g, carry):
            forward_own(c, g).wait()
            for d in range(1, cols):
                forward_copy(c, g, d, True).wait_recv()
            for k in range(group):
                t = g * group + k
                for j in range(0, SUB, 2):
                    pair = left_pair(xf[...], *(
                        jnp.concatenate([frecv[q, c, t, i * block : (i + 1) * block, :] for q in range(cols)], axis=0)
                        for i in (j, j + 1)
                    ))
                    for k2, value in enumerate(pair):
                        modal[t, (j + k2) * nx : (j + k2 + 1) * nx] = value
            return carry

        lax.fori_loop(0, rows // group, arrive, 0)

        def maps(j, carry):
            own = pl.ds(pl.multiple_of(j * nx, nx), nx)
            g = modal[0, own] * rd[c, 0, own]
            for t in range(1, rows):
                g = modal[t, own] * rd[c, t, own] + w[c, t, own] * g
            maps_own[c, j, 0] = g
            h = modal[rows - 1, own] * rdb[c, rows - 1, own]
            for t in range(rows - 2, -1, -1):
                h = modal[t, own] * rdb[c, t, own] + wb[c, t, own] * h
            maps_own[c, j, 1] = h
            maps_copy(c, j).start()
            return carry

        lax.fori_loop(0, SUB, maps, 0)

        def finish(j):
            own = pl.ds(pl.multiple_of(j * nx, nx), nx)
            g = jnp.where(side == 0, gr[c, j], gin[c, j])
            later = jnp.where(side == 1, hr[c, j], hin[c, j])
            for t in range(rows):
                g = modal[t, own] * rd[c, t, own] + w[c, t, own] * g
                modal[t, own] = g
            value, waiting = None, []
            for t in range(rows - 1, -1, -1):
                if value is None:
                    value = (g - e[c, t, own] * later) * last[c, j]
                else:
                    value = modal[t, own] - e[c, t, own] * value
                waiting.append((t, value))
                if len(waiting) == 2 or t == 0:
                    if len(waiting) == 2:
                        done = left_pair(xb[...], waiting[0][1], waiting[1][1])
                    else:
                        done = (left(xb[...], value),)
                    for (t2, _), back in zip(waiting, done):
                        at = pl.ds(pl.multiple_of((j * rows + t2) * block, block), block)
                        for q in range(cols):
                            bsend[q, c, at] = back[q * block : (q + 1) * block]
                    waiting = []
            for d in range(1, cols):
                back_copy(c, j, d, False).start()
            back_own(c, j).start()

        def tick(n, carry):
            @pl.when(n < SUB)
            def _():
                maps_copy(c, n).wait_recv()

            j = n - WAVE * level

            @pl.when((j >= 0) & (j < SUB))
            def _():
                @pl.when(level > 0)
                def _():
                    upward(c, j).wait_recv()

                carried = gr[c, j]
                kept, passed = maps_own[c, j, 0], maps_other[c, j, 0]
                kept_step, passed_step = steps_own[c, j, 0], steps_other[c, j, 0]

                @pl.when(side == 0)
                def _():
                    gs[c, j] = passed + passed_step * (kept + kept_step * carried)

                @pl.when(side == 1)
                def _():
                    inner = passed + passed_step * carried
                    gin[c, j] = inner
                    gs[c, j] = kept + kept_step * inner

                @pl.when(level < levels - 1)
                def _():
                    upward(c, j).start()

            i = n - WAVE * (levels - 1 - level)

            @pl.when((i >= 0) & (i < SUB))
            def _():
                @pl.when(level < levels - 1)
                def _():
                    downward(c, i).wait_recv()

                carried = hr[c, i]
                kept, passed = maps_own[c, i, 1], maps_other[c, i, 1]
                kept_step, passed_step = steps_own[c, i, 1], steps_other[c, i, 1]

                @pl.when(side == 1)
                def _():
                    hs[c, i] = passed + passed_step * (kept + kept_step * carried)

                @pl.when(side == 0)
                def _():
                    inner = passed + passed_step * carried
                    hin[c, i] = inner
                    hs[c, i] = kept + kept_step * inner

                @pl.when(level > 0)
                def _():
                    downward(c, i).start()

            f = n - WAVE * jnp.maximum(level, levels - 1 - level)

            @pl.when((f >= 0) & (f < SUB))
            def _():
                finish(f)

            return carry

        lax.fori_loop(0, WAVE * (levels - 1) + SUB, tick, 0)

        return carry

    lax.fori_loop(0, chunks, chunk, 0)

    def store(c, j):
        part = pl.ds(pl.multiple_of(j * rows * block, rows * block), rows * block)
        return pltpu.make_async_copy(brecv.at[:, c, part], out_ref.at[:, c, part], out_sem.at[c, j])

    def zstage(n, carry):
        c, j = n // SUB, lax.rem(n, SUB)
        back_own(c, j).wait()
        for d in range(1, cols):
            back_copy(c, j, d, True).wait_recv()
        part = pl.ds(pl.multiple_of(j * rows * block, rows * block), rows * block)
        for q in range(cols):
            brecv[q, c, part] = right(brecv[q, c, part], zb1[...], zb2[...])
        store(c, j).start()
        return carry

    lax.fori_loop(0, span, zstage, 0)

    for c in range(chunks):
        for g in range(rows // group):
            for d in range(1, cols):
                forward_copy(c, g, d, False).wait_send()

    def drain(n, carry):
        c, j = n // SUB, lax.rem(n, SUB)
        for d in range(1, cols):
            back_copy(c, j, d, False).wait_send()

        maps_copy(c, j).wait_send()

        @pl.when(level < levels - 1)
        def _():
            upward(c, j).wait_send()

        @pl.when(level > 0)
        def _():
            downward(c, j).wait_send()

        return carry

    lax.fori_loop(0, span, drain, 0)
    for n in range(span):
        store(n // SUB, n % SUB).wait()


def last_stage(basis_y, field, out_ref):
    basis = tripled(basis_y[...])
    cols, chunks, _, _, block, nz = field.shape
    for a in range(0, block, 2):
        out_ref[0, a], out_ref[0, a + 1] = left_pair(basis, *(
            jnp.concatenate([field[q, c, :, 0, i, :] for q in range(cols) for c in range(chunks)], axis=0)
            for i in (a, a + 1)
        ))


def local(chain, cols, right_side, basis_x, basis_y, basis_z, eig_x, eig_y, eig_z, steps):
    rows, block, ny, nz = right_side.shape
    nx = basis_x.shape[0]
    total = steps.shape[0]
    chunks = ny // cols // SUB
    group = 1
    vmem, smem, anywhere = (
        pl.BlockSpec(memory_space=pltpu.VMEM),
        pl.BlockSpec(memory_space=pltpu.SMEM),
        pl.BlockSpec(memory_space=pl.ANY),
    )
    modes = SUB * nx
    dma = pltpu.SemaphoreType.DMA
    table = pltpu.VMEM((chunks, rows, modes, nz), F32)
    tile = pltpu.VMEM((chunks, SUB, nx, nz), F32)
    twin = pltpu.VMEM((chunks, SUB, 2, nx, nz), F32)
    travel = pltpu.VMEM((cols, chunks, rows, SUB * block, nz), F32)
    back = pltpu.VMEM((cols, chunks, SUB * rows * block, nz), F32)
    groups = rows // group
    field = pl.pallas_call(
        partial(kernel, chain, cols, chunks, group),
        out_shape=jax.ShapeDtypeStruct((cols, chunks, SUB * rows * block, nz), F32),
        in_specs=[anywhere] + [vmem] * 5 + [smem] * 2,
        out_specs=anywhere,
        scratch_shapes=[
            pltpu.VMEM((2 * nz, nz), BF), pltpu.VMEM((nz, nz), BF), pltpu.VMEM((2 * nz, nz), BF), pltpu.VMEM((nz, nz), BF),
            pltpu.VMEM((ny, 3 * ny), BF), pltpu.VMEM((ny, 3 * ny), BF),
            pltpu.VMEM((nx, 3 * nx), BF), pltpu.VMEM((nx, 3 * nx), BF), pltpu.VMEM((nx, nz), F32),
            pltpu.SMEM((total,), F32), pltpu.SMEM((total + 1,), F32), pltpu.SMEM((total + 1,), F32),
            pltpu.VMEM((rows, block, ny, nz), F32), travel, travel, pltpu.VMEM((rows, modes, nz), F32),
            table, table, table, table, table, tile, twin, twin, twin, twin,
            tile, tile, tile, tile, tile, tile, back, back,
            dma((rows,)), dma((chunks, SUB)),
            dma((chunks, groups, cols - 1)), dma((chunks, groups, cols - 1)), dma((chunks, groups)),
            dma((chunks, SUB, cols - 1)), dma((chunks, SUB, cols - 1)), dma((chunks, SUB)),
            dma((chunks, SUB)), dma((chunks, SUB)), dma((chunks, SUB)), dma((chunks, SUB)),
            dma((chunks, SUB)), dma((chunks, SUB)),
        ],
        compiler_params=pltpu.CompilerParams(
            collective_id=0, has_side_effects=True, vmem_limit_bytes=60 * 1024 * 1024
        ),
    )(
        right_side, basis_x, basis_y, basis_z, eig_x.reshape(1, nx), eig_z.reshape(1, nz), eig_y, steps
    )
    return pl.pallas_call(
        last_stage,
        grid=(rows,),
        out_shape=jax.ShapeDtypeStruct(right_side.shape, F32),
        in_specs=[
            pl.BlockSpec((ny, ny), lambda t: (0, 0)),
            pl.BlockSpec((cols, chunks, SUB, 1, block, nz), lambda t: (0, 0, 0, t, 0, 0)),
        ],
        out_specs=pl.BlockSpec((1, block, ny, nz), lambda t: (t, 0, 0, 0)),
    )(basis_y, field.reshape(cols, chunks, SUB, rows, block, nz))


def solution(mesh):
    return jax.shard_map(
        partial(local, mesh.shape["ta"], mesh.shape["gx"]),
        mesh=mesh,
        in_specs=(P("ta", "gx", None, None), P(), P(), P(), P(), P(), P(), P()),
        out_specs=P("ta", "gx", None, None),
        check_vma=False,
    )
```
